256 devices in a mesh: row: 32 (over z_lo, y, core), col: 8 (over x, z_hi).
Axes of the slice: x: 4, y: 4, z: 8 (z_hi: 2, z_lo: 4; z = z_hi * 4 + z_lo), core: 2. Of those that a mesh axis runs over, the one named last changes fastest.
Arguments:
- stem_slab: float32 [2, 256, 256, 1024], P(None, 'row', None, 'col'), may hold values from -6 to 6
- factors: float32 [256, 2, 2, 256, 256], P(('row', 'col')), may hold values from -0.25 to 0.25
- branch_owner: int32 [4], replicated, may hold values from 0 to 255
- entangle_phase: float32 [4, 256, 256], replicated, may hold values from -3.140625 to 3.140625
Outputs:
- contracted: float32 [2, 256, 256, 1024], P(None, 'row', None, 'col')
The draws below stay inside these ranges and needn't reach their ends.
All inputs are finite; a program needn't handle non-finite values.
Results may differ from the reference program's by a relative error of at most 0.000039.
Values sent between devices are 32-bit elements; how exact they have to be, the bound alone decides.
A program may use at most 64 MiB of HBM per device.

```python
from functools import partial
import jax
import jax.numpy as jnp
from jax import lax

W = 256
STEPS = 4
NBATCH = 1024
DEVICES_ALL = 256
N_ROW = 32
N_COL = 8


def plant(drawn, rng, smallest, high):
    dims = drawn.shape
    index_at = [jax.random.randint(jax.random.fold_in(rng, axis), (), 0, dims[axis]) for axis in range(len(dims))]
    drawn = drawn.at[tuple(index_at)].set(smallest)
    longest = dims.index(max(dims))
    index_at[longest] = (index_at[longest] + 1) % dims[longest]
    return drawn.at[tuple(index_at)].set(high)


def shard_levels(rng, dims, split, least, largest):
    def one(axis_at, shards_of):
        draws = jax.random.uniform(jax.random.fold_in(jax.random.fold_in(rng, 6), axis_at), (shards_of,), jnp.float32, least / len(split), largest / len(split))
        return jnp.repeat(jnp.exp(draws), dims[axis_at] // shards_of).reshape((-1,) + (1,) * (len(dims) - axis_at - 1))

    level = one(*split[0])
    for cut in split[1:]:
        level = level * one(*cut)
    return level


def gaussian(rng, shape, scale, reach, split=(), dtype=jnp.bfloat16):
    loudness = shard_levels(rng, shape, split, -0.22, 0.18) if split else 1.0
    values = jax.random.normal(rng, shape, jnp.float32) * scale * loudness
    return jnp.minimum(jnp.maximum(values, -reach), reach).astype(dtype)


def setup_inputs(seed: int = 0) -> dict:
    key_of = jax.random.split(jax.random.key(seed), 5)
    return {
        "stem_slab": gaussian(key_of[0], (2, W, W, NBATCH), 1.0, 6.0, ((1, 32), (3, 8)), jnp.float32),
        "factors": gaussian(key_of[1], (DEVICES_ALL, 2, 2, W, W), (2 * W) ** -0.5, 0.25, ((0, 256),), jnp.float32),
        "branch_owner": plant(jax.random.randint(key_of[2], (STEPS,), 0, N_ROW * N_COL), jax.random.fold_in(key_of[2], 1), 0, (N_ROW * N_COL) - 1).astype(jnp.int32),
        "entangle_phase": jnp.clip(jax.random.uniform(key_of[3], (STEPS, W, W), jnp.float32, -3.140625, 3.140625), -3.140625, 3.140625),
    }


def complex_mix(real_part, imag_part, branch_real, branch_imag, form):
    mix = partial(jnp.einsum, form, precision=lax.Precision.HIGHEST)
    return (mix(real_part, branch_real) - mix(imag_part, branch_imag),
            mix(real_part, branch_imag) + mix(imag_part, branch_real))


def build_branch(owned):
    dot_high = partial(jnp.dot, precision=lax.Precision.HIGHEST)
    left_real, left_imag = owned[0, 0], owned[0, 1]
    right_real, right_imag = owned[1, 0], owned[1, 1]
    return (dot_high(left_real, right_real) - dot_high(left_imag, right_imag),
            dot_high(left_real, right_imag) + dot_high(left_imag, right_real))


def reference(stem_slab, factors, branch_owner, entangle_phase):
    real_part, imag_part = stem_slab[0], stem_slab[1]
    for step in range(STEPS):
        owned = lax.dynamic_index_in_dim(factors, branch_owner[step].astype(jnp.int32), 0, keepdims=False)
        branch_real, branch_imag = build_branch(owned)
        if step % 2 == 0:
            real_part, imag_part = complex_mix(real_part, imag_part, branch_real, branch_imag, "akb,kl->alb")
        else:
            real_part, imag_part = complex_mix(real_part, imag_part, branch_real, branch_imag, "akb,al->lkb")
        cosine = jnp.cos(entangle_phase[step])[:, :, None]
        sine = jnp.sin(entangle_phase[step])[:, :, None]
        real_part, imag_part = (real_part * cosine - imag_part * sine,
                                real_part * sine + imag_part * cosine)
    return jnp.stack([real_part, imag_part])
```

```python
import functools

import jax
import jax.numpy as jnp
from jax import lax
from jax.experimental import pallas as pl
from jax.experimental.pallas import tpu as pltpu
from jax.sharding import PartitionSpec as P

MESH = pl.DeviceIdType.MESH
F32 = jnp.float32
BF16 = jnp.bfloat16
STEPS = 4

NX, NY, NZ, NC = 4, 4, 8, 2
N_ROW = 32
BATCHES = ((1, 8), (8, 16), (16, 17), (17, 18), (18, 19), (19, 32))


def split(value):
    high = value.astype(BF16)
    return high, (value - high.astype(F32)).astype(BF16)


def dot3(left, right):
    (lh, ll), (rh, rl) = left, right
    dot = functools.partial(jnp.dot, preferred_element_type=F32)
    return dot(lh, rh) + (dot(lh, rl) + dot(ll, rh))


def drained(ref, sem):
    pltpu.make_async_copy(ref, ref, sem).wait()


def kernel(
    owner, factors, stem, phase, out,
    recv, mixed, cosine, sine, own, raw0, raw1, slots, from_y, summed, from_z, full,
    high, low, send, land, a_send, a_land, b_send, b_land, local,
):
    row, col = lax.axis_index("row"), lax.axis_index("col")
    core, y, z_lo = row % 2, (row // 2) % 4, row // 8
    x, z_hi = col // 2, col % 2
    z = z_hi * 4 + z_lo

    def at_core(c):
        return (z_lo * 8 + y * 2 + c, col)

    def at_x(i):
        return (row, i * 2 + z_hi)

    def at_y(i):
        return (z_lo * 8 + i * 2 + core, col)

    def at_z(i):
        return ((i % 4) * 8 + y * 2 + core, x * 2 + i // 4)

    def row_peer(i):
        peer = ((z_lo + i % 4) % 4) * 8 + (row + i // 4) % 8
        return peer

    barrier = pltpu.get_barrier_semaphore()

    def greet(device):
        pl.semaphore_signal(barrier, inc=1, device_id=device, device_id_type=MESH)

    @pl.loop(1, N_ROW)
    def _(i):
        greet((row_peer(i), col))

    @pl.loop(1, NX)
    def _(i):
        greet(at_x((x + i) % NX))

    @pl.loop(0, NZ // 2)
    def _(i):
        greet(at_z((1 - z_hi) * 4 + i))

    dot = functools.partial(jnp.dot, precision=lax.Precision.HIGHEST, preferred_element_type=F32)
    own[0] = dot(factors[0, 0], factors[1, 0]) - dot(factors[0, 1], factors[1, 1])
    own[1] = dot(factors[0, 0], factors[1, 1]) + dot(factors[0, 1], factors[1, 0])

    pl.semaphore_wait(barrier, N_ROW - 1 + NX - 1 + NZ // 2)

    def push(src, dst, stage, device):
        pltpu.make_async_remote_copy(
            src_ref=src, dst_ref=dst, send_sem=send.at[stage], recv_sem=land.at[stage],
            device_id=device, device_id_type=MESH,
        ).start()

    def stem_batch(first, last):
        @pl.loop(first, last)
        def _(i):
            peer = row_peer(i)
            pltpu.make_async_remote_copy(
                src_ref=stem.at[:, pl.ds(peer * 4, 4)],
                dst_ref=recv.at[:, :, pl.ds(row * 8, 8)],
                send_sem=a_send, recv_sem=a_land,
                device_id=(peer, col), device_id_type=MESH,
            ).start()

    push(own.at[1 - core], raw0.at[core], 0, at_core(1 - core))
    keep = pltpu.make_async_copy(
        stem.at[:, pl.ds(row * 4, 4)], recv.at[:, :, pl.ds(row * 8, 8)], local.at[0]
    )
    keep.start()
    stem_batch(*BATCHES[0])
    raw0[core] = own[core]
    drained(raw0.at[0], land.at[0])

    @pl.loop(1, NX)
    def _(i):
        peer = (x + i) % NX
        push(raw0.at[:, pl.ds(peer * 64, 64)], raw1.at[x], 1, at_x(peer))

    stem_batch(*BATCHES[1])
    raw1[x] = raw0[:, pl.ds(x * 64, 64)]

    @pl.loop(0, STEPS)
    def _(step):
        @pl.loop(0, 32)
        def _(i):
            angle = phase[step, pl.ds(i * 8, 8)]
            cosine[step, pl.ds(i * 8, 8)] = jnp.cos(angle)
            sine[step, pl.ds(i * 8, 8)] = jnp.sin(angle)

    drained(raw1.at[pl.ds(0, NX - 1)], land.at[1])
    for step in range(STEPS):
        at = owner[step]
        at_row, at_col = lax.shift_right_logical(at, 3), at & 7
        at_z_y = (at_col & 1) * 4 + lax.shift_right_logical(at_row, 3), lax.shift_right_logical(at_row, 1) & 3
        here = jnp.logical_and(at_z_y[0] == z, at_z_y[1] == y)
        value = raw1[lax.shift_right_logical(at_col, 1), at_row & 1]
        slots[step] = jnp.where(here, value, jnp.zeros_like(value))

    @pl.loop(1, NY)
    def _(i):
        peer = (y + i) % NY
        push(slots.at[:, pl.ds(peer * 16, 16)], from_y.at[y], 2, at_y(peer))

    stem_batch(*BATCHES[2])
    from_y[y] = slots[:, pl.ds(y * 16, 16)]
    drained(from_y.at[pl.ds(0, NY - 1)], land.at[2])
    total = (from_y[0] + from_y[1]) + (from_y[2] + from_y[3])
    summed[...] = total.reshape(NZ, 8, 256)

    @pl.loop(1, NZ)
    def _(i):
        peer = (z + i) % NZ
        push(summed.at[peer], from_z.at[z], 3, at_z(peer))

    stem_batch(*BATCHES[3])
    from_z[z] = summed[z]
    drained(from_z.at[pl.ds(0, NZ - 1)], land.at[3])
    total = from_z[0]
    for i in range(1, NZ):
        total = total + from_z[i]
    mine = full.at[:, core, x, y]
    eighth = full.at[z // 2, core, x, y, z % 2]
    eighth[...] = total

    @pl.loop(1, NZ)
    def _(i):
        push(eighth, eighth, 4, at_z((z + i) % NZ))

    stem_batch(*BATCHES[4])
    drained(from_z.at[pl.ds(0, NZ - 1)], land.at[4])

    @pl.loop(1, NY)
    def _(i):
        push(mine, mine, 5, at_y((y + i) % NY))

    drained(from_y.at[pl.ds(0, NY - 1)], land.at[5])
    quarter = full.at[:, core, x]

    @pl.loop(1, NX)
    def _(i):
        push(quarter, quarter, 6, at_x((x + i) % NX))

    stem_batch(*BATCHES[5])
    drained(full.at[pl.ds(0, NX - 1), 0], land.at[6])
    half = full.at[:, core]
    push(half, half, 7, at_core(1 - core))
    drained(half, land.at[7])

    for step in range(STEPS):
        for part in range(2):
            branch = full[step, part].reshape(256, 256)
            if step % 2:
                branch = branch.T
            high[step, part], low[step, part] = split(branch)

    keep.wait()
    drained(stem.at[:, pl.ds(0, (N_ROW - 1) * 4)], a_land)

    @pl.loop(0, 4)
    def _(b):
        real, imag = recv[0, b], recv[1, b]
        for step in range(STEPS):
            xr, xi = split(real), split(imag)
            br = (high[step, 0], low[step, 0])
            bi = (high[step, 1], low[step, 1])
            if step % 2:
                yr = dot3(br, xr) - dot3(bi, xi)
                yi = dot3(bi, xr) + dot3(br, xi)
            else:
                yr = dot3(xr, br) - dot3(xi, bi)
                yi = dot3(xr, bi) + dot3(xi, br)
            real = yr * cosine[step] - yi * sine[step]
            imag = yr * sine[step] + yi * cosine[step]
        mixed[b, 0] = real
        mixed[b, 1] = imag
        pltpu.make_async_copy(
            mixed.at[b, :, pl.ds(row * 8, 8)], out.at[:, row * 4 + b], local.at[1]
        ).start()

        @pl.loop(1, N_ROW)
        def _(i):
            peer = row_peer(i)
            pltpu.make_async_remote_copy(
                src_ref=mixed.at[b, :, pl.ds(peer * 8, 8)],
                dst_ref=out.at[:, row * 4 + b],
                send_sem=b_send, recv_sem=b_land,
                device_id=(peer, col), device_id_type=MESH,
            ).start()

    drained(out.at[:, pl.ds(0, 4)], local.at[1])
    drained(out.at[:, pl.ds(0, (N_ROW - 1) * 4)], b_land)
    drained(raw0.at[0], send.at[0])
    drained(raw1.at[pl.ds(0, NX - 1)], send.at[1])
    drained(from_y.at[pl.ds(0, NY - 1)], send.at[2])
    drained(from_z.at[pl.ds(0, NZ - 1)], send.at[3])
    drained(from_z.at[pl.ds(0, NZ - 1)], send.at[4])
    drained(from_y.at[pl.ds(0, NY - 1)], send.at[5])
    drained(full.at[pl.ds(0, NX - 1), 0], send.at[6])
    drained(full.at[:, 0], send.at[7])
    drained(stem.at[:, pl.ds(0, (N_ROW - 1) * 4)], a_send)
    drained(out.at[:, pl.ds(0, (N_ROW - 1) * 4)], b_send)


def on_device(stem_slab, factors, branch_owner, entangle_phase):
    stem = stem_slab.transpose(0, 3, 1, 2)
    vmem, dma = pltpu.VMEM, pltpu.SemaphoreType.DMA
    out = pl.pallas_call(
        kernel,
        out_shape=jax.ShapeDtypeStruct((2, 128, 8, 256), F32),
        in_specs=[
            pl.BlockSpec(memory_space=pltpu.SMEM),
            pl.BlockSpec(memory_space=pltpu.VMEM),
            pl.BlockSpec(memory_space=pl.ANY),
            pl.BlockSpec(memory_space=pltpu.VMEM),
        ],
        out_specs=pl.BlockSpec(memory_space=pl.ANY),
        scratch_shapes=[
            vmem((2, 4, 256, 256), F32),
            vmem((4, 2, 256, 256), F32),
            vmem((4, 256, 256), F32),
            vmem((4, 256, 256), F32),
            vmem((2, 256, 256), F32),
            vmem((2, 256, 256), F32),
            vmem((4, 2, 64, 256), F32),
            vmem((4, 64, 256), F32),
            vmem((4, 4, 16, 256), F32),
            vmem((8, 8, 256), F32),
            vmem((8, 8, 256), F32),
            vmem((4, 2, 4, 4, 2, 8, 256), F32),
            vmem((4, 2, 256, 256), BF16),
            vmem((4, 2, 256, 256), BF16),
            dma((8,)), dma((8,)),
            dma(()), dma(()), dma(()), dma(()),
            dma((2,)),
        ],
        compiler_params=pltpu.CompilerParams(collective_id=0, has_side_effects=True),
    )(branch_owner, factors[0], stem, entangle_phase)
    return out.transpose(0, 2, 3, 1)


def solution(mesh):
    return jax.shard_map(
        on_device,
        mesh=mesh,
        in_specs=(P(None, "row", None, "col"), P(("row", "col"), None, None, None, None), P(), P()),
        out_specs=P(None, "row", None, "col"),
        check_vma=False,
    )
```

```python
import functools

import jax
import jax.numpy as jnp
from jax import lax
from jax.experimental import pallas as pl
from jax.experimental.pallas import tpu as pltpu
from jax.sharding import PartitionSpec as P

MESH = pl.DeviceIdType.MESH
F32 = jnp.float32
BF16 = jnp.bfloat16
STEPS = 4

NX, NY, NZ, NC = 4, 4, 8, 2
N_ROW = 32
PEERS = N_ROW - 1
BATCHES = (0, 12, 36, 48, 60, 72, 90, 124)


def split(value):
    high = value.astype(BF16)
    return high, (value - high.astype(F32)).astype(BF16)


def dot3(left, right):
    (lh, ll), (rh, rl) = left, right
    dot = functools.partial(jnp.dot, preferred_element_type=F32)
    return dot(lh, rh) + (dot(lh, rl) + dot(ll, rh))


def drained(ref, sem):
    pltpu.make_async_copy(ref, ref, sem).wait()


def kernel(
    owner, factors_hbm, stem_hbm, phase_hbm, out,
    factors, stem, phase, turned, recv, mixed, cosine, sine, own, raw0, raw1, slots, from_y, summed, from_z, full,
    high, low, send, land, a_send, a_land, b_send, b_land, local,
):
    row, col = lax.axis_index("row"), lax.axis_index("col")
    core, y, z_lo = row % 2, (row // 2) % 4, row // 8
    x, z_hi = col // 2, col % 2
    z = z_hi * 4 + z_lo

    def at_core(c):
        return (z_lo * 8 + y * 2 + c, col)

    def at_x(i):
        return (row, i * 2 + z_hi)

    def at_y(i):
        return (z_lo * 8 + i * 2 + core, col)

    def at_z(i):
        return ((i % 4) * 8 + y * 2 + core, x * 2 + i // 4)

    def row_peer(i):
        peer = ((z_lo + i % 4) % 4) * 8 + (row + i // 4) % 8
        return peer

    loads = [
        pltpu.make_async_copy(stem_hbm.at[0], stem.at[0], local.at[0]),
        pltpu.make_async_copy(stem_hbm.at[1], stem.at[1], local.at[1]),
        pltpu.make_async_copy(factors_hbm, factors, local.at[2]),
        pltpu.make_async_copy(phase_hbm, phase, local.at[3]),
    ]
    for load in loads:
        load.start()

    barrier = pltpu.get_barrier_semaphore()

    def greet(device):
        pl.semaphore_signal(barrier, inc=1, device_id=device, device_id_type=MESH)

    @pl.loop(1, N_ROW)
    def _(i):
        greet((row_peer(i), col))

    @pl.loop(1, NX)
    def _(i):
        greet(at_x((x + i) % NX))

    @pl.loop(0, NZ // 2)
    def _(i):
        greet(at_z((1 - z_hi) * 4 + i))

    for part in range(2):
        loads[part].wait()

        @pl.loop(0, 8)
        def _(a):
            for i in range(2):
                turned[part, i, pl.ds(a, 128, stride=8)] = stem[part, a, pl.ds(i * 128, 128)].T

    loads[2].wait()
    dot = functools.partial(jnp.dot, precision=lax.Precision.HIGHEST, preferred_element_type=F32)
    own[0] = dot(factors[0, 0], factors[1, 0]) - dot(factors[0, 1], factors[1, 1])
    own[1] = dot(factors[0, 0], factors[1, 1]) + dot(factors[0, 1], factors[1, 0])

    pl.semaphore_wait(barrier, N_ROW - 1 + NX - 1 + NZ // 2)

    def push(src, dst, stage, device):
        pltpu.make_async_remote_copy(
            src_ref=src, dst_ref=dst, send_sem=send.at[stage], recv_sem=land.at[stage],
            device_id=device, device_id_type=MESH,
        ).start()

    def stem_batch(index):
        @pl.loop(BATCHES[index], BATCHES[index + 1])
        def _(i):
            peer, b = row_peer(1 + i % PEERS), i // PEERS
            pltpu.make_async_remote_copy(
                src_ref=turned.at[:, :, pl.ds((peer * 4 + b) * 8, 8)],
                dst_ref=recv.at[:, b, :, pl.ds(row * 8, 8)],
                send_sem=a_send, recv_sem=a_land.at[b],
                device_id=(peer, col), device_id_type=MESH,
            ).start()

    push(own.at[1 - core], raw0.at[core], 0, at_core(1 - core))
    stem_batch(0)
    raw0[core] = own[core]
    for b in range(4):
        recv[:, b, :, pl.ds(row * 8, 8)] = turned[:, :, pl.ds((row * 4 + b) * 8, 8)]

    drained(raw0.at[0], land.at[0])

    @pl.loop(1, NX)
    def _(i):
        peer = (x + i) % NX
        push(raw0.at[:, pl.ds(peer * 64, 64)], raw1.at[x], 1, at_x(peer))

    stem_batch(1)
    raw1[x] = raw0[:, pl.ds(x * 64, 64)]
    loads[3].wait()

    @pl.loop(0, STEPS)
    def _(step):
        @pl.loop(0, 32)
        def _(i):
            angle = phase[step, pl.ds(i * 8, 8)]
            cosine[step, pl.ds(i * 8, 8)] = jnp.cos(angle)
            sine[step, pl.ds(i * 8, 8)] = jnp.sin(angle)

    drained(raw1.at[pl.ds(0, NX - 1)], land.at[1])
    for step in range(STEPS):
        at = owner[step]
        at_row, at_col = lax.shift_right_logical(at, 3), at & 7
        at_z_y = (at_col & 1) * 4 + lax.shift_right_logical(at_row, 3), lax.shift_right_logical(at_row, 1) & 3
        here = jnp.logical_and(at_z_y[0] == z, at_z_y[1] == y)
        value = raw1[lax.shift_right_logical(at_col, 1), at_row & 1]
        slots[step] = jnp.where(here, value, jnp.zeros_like(value))

    @pl.loop(1, NY)
    def _(i):
        peer = (y + i) % NY
        push(slots.at[:, pl.ds(peer * 16, 16)], from_y.at[y], 2, at_y(peer))

    stem_batch(2)
    from_y[y] = slots[:, pl.ds(y * 16, 16)]
    drained(from_y.at[pl.ds(0, NY - 1)], land.at[2])
    total = (from_y[0] + from_y[1]) + (from_y[2] + from_y[3])
    summed[...] = total.reshape(NZ, 8, 256)

    @pl.loop(1, NZ)
    def _(i):
        peer = (z + i) % NZ
        push(summed.at[peer], from_z.at[z], 3, at_z(peer))

    stem_batch(3)
    from_z[z] = summed[z]
    drained(from_z.at[pl.ds(0, NZ - 1)], land.at[3])
    total = from_z[0]
    for i in range(1, NZ):
        total = total + from_z[i]
    mine = full.at[:, core, x, y]
    eighth = full.at[z // 2, core, x, y, z % 2]
    eighth[...] = total

    @pl.loop(1, NZ)
    def _(i):
        push(eighth, eighth, 4, at_z((z + i) % NZ))

    stem_batch(4)
    drained(from_z.at[pl.ds(0, NZ - 1)], land.at[4])

    @pl.loop(1, NY)
    def _(i):
        push(mine, mine, 5, at_y((y + i) % NY))

    stem_batch(5)
    drained(from_y.at[pl.ds(0, NY - 1)], land.at[5])
    quarter = full.at[:, core, x]

    @pl.loop(1, NX)
    def _(i):
        push(quarter, quarter, 6, at_x((x + i) % NX))

    stem_batch(6)
    drained(full.at[pl.ds(0, NX - 1), 0], land.at[6])
    half = full.at[:, core]
    push(half, half, 7, at_core(1 - core))
    drained(half, land.at[7])

    for step in range(STEPS):
        for part in range(2):
            branch = full[step, part].reshape(256, 256)
            if step % 2:
                branch = branch.T
            high[step, part], low[step, part] = split(branch)


    @pl.loop(0, 4)
    def _(b):
        drained(turned.at[:, :, pl.ds(0, PEERS * 8)], a_land.at[b])
        real = jnp.concatenate([recv[0, b, 0], recv[0, b, 1]], axis=1)
        imag = jnp.concatenate([recv[1, b, 0], recv[1, b, 1]], axis=1)
        for step in range(STEPS):
            xr, xi = split(real), split(imag)
            br = (high[step, 0], low[step, 0])
            bi = (high[step, 1], low[step, 1])
            if step % 2:
                yr = dot3(br, xr) - dot3(bi, xi)
                yi = dot3(bi, xr) + dot3(br, xi)
            else:
                yr = dot3(xr, br) - dot3(xi, bi)
                yi = dot3(xr, bi) + dot3(xi, br)
            real = yr * cosine[step] - yi * sine[step]
            imag = yr * sine[step] + yi * cosine[step]
        mixed[b, 0] = real
        mixed[b, 1] = imag
        pltpu.make_async_copy(
            mixed.at[b, :, pl.ds(row * 8, 8)], out.at[:, row * 4 + b], local.at[4]
        ).start()

        @pl.loop(1, N_ROW)
        def _(i):
            peer = row_peer(i)
            pltpu.make_async_remote_copy(
                src_ref=mixed.at[b, :, pl.ds(peer * 8, 8)],
                dst_ref=out.at[:, row * 4 + b],
                send_sem=b_send, recv_sem=b_land,
                device_id=(peer, col), device_id_type=MESH,
            ).start()

    drained(out.at[:, pl.ds(0, 4)], local.at[4])
    drained(out.at[:, pl.ds(0, PEERS * 4)], b_land)
    drained(raw0.at[0], send.at[0])
    drained(raw1.at[pl.ds(0, NX - 1)], send.at[1])
    drained(from_y.at[pl.ds(0, NY - 1)], send.at[2])
    drained(from_z.at[pl.ds(0, NZ - 1)], send.at[3])
    drained(from_z.at[pl.ds(0, NZ - 1)], send.at[4])
    drained(from_y.at[pl.ds(0, NY - 1)], send.at[5])
    drained(full.at[pl.ds(0, NX - 1), 0], send.at[6])
    drained(full.at[:, 0], send.at[7])
    drained(turned.at[:, :, pl.ds(0, PEERS * 32)], a_send)
    drained(out.at[:, pl.ds(0, PEERS * 4)], b_send)


def on_device(stem_slab, factors, branch_owner, entangle_phase):
    vmem, dma = pltpu.VMEM, pltpu.SemaphoreType.DMA
    out = pl.pallas_call(
        kernel,
        out_shape=jax.ShapeDtypeStruct((2, 128, 8, 256), F32),
        in_specs=[
            pl.BlockSpec(memory_space=pltpu.SMEM),
            pl.BlockSpec(memory_space=pl.ANY),
            pl.BlockSpec(memory_space=pl.ANY),
            pl.BlockSpec(memory_space=pl.ANY),
        ],
        out_specs=pl.BlockSpec(memory_space=pl.ANY),
        scratch_shapes=[
            vmem((2, 2, 256, 256), F32),
            vmem((2, 8, 256, 128), F32),
            vmem((4, 256, 256), F32),
            vmem((2, 2, 1024, 128), F32),
            vmem((2, 4, 2, 256, 128), F32),
            vmem((4, 2, 256, 256), F32),
            vmem((4, 256, 256), F32),
            vmem((4, 256, 256), F32),
            vmem((2, 256, 256), F32),
            vmem((2, 256, 256), F32),
            vmem((4, 2, 64, 256), F32),
            vmem((4, 64, 256), F32),
            vmem((4, 4, 16, 256), F32),
            vmem((8, 8, 256), F32),
            vmem((8, 8, 256), F32),
            vmem((4, 2, 4, 4, 2, 8, 256), F32),
            vmem((4, 2, 256, 256), BF16),
            vmem((4, 2, 256, 256), BF16),
            dma((8,)), dma((8,)),
            dma(()), dma((4,)), dma(()), dma(()),
            dma((5,)),
        ],
        compiler_params=pltpu.CompilerParams(collective_id=0, has_side_effects=True),
    )(branch_owner, factors[0], stem_slab, entangle_phase)
    return out.transpose(0, 2, 3, 1)


def solution(mesh):
    return jax.shard_map(
        on_device,
        mesh=mesh,
        in_specs=(P(None, "row", None, "col"), P(("row", "col"), None, None, None, None), P(), P()),
        out_specs=P(None, "row", None, "col"),
        check_vma=False,
    )
```

```python
import functools

import jax
import jax.numpy as jnp
from jax import lax
from jax.experimental import pallas as pl
from jax.experimental.pallas import tpu as pltpu
from jax.sharding import PartitionSpec as P

MESH = pl.DeviceIdType.MESH
F32 = jnp.float32
BF16 = jnp.bfloat16
STEPS = 4

NX, NY, NZ, NC = 4, 4, 8, 2
N_ROW = 32
PEERS = N_ROW - 1
EARLY = 1
BATCHES = (0, 12, 36, 48, 60, 72, 90, 124)


def split(value):
    high = value.astype(BF16)
    return high, (value - high.astype(F32)).astype(BF16)


def dot3(left, right):
    (lh, ll), (rh, rl) = left, right
    dot = functools.partial(jnp.dot, preferred_element_type=F32)
    return dot(lh, rh) + (dot(lh, rl) + dot(ll, rh))


def drained(ref, sem):
    pltpu.make_async_copy(ref, ref, sem).wait()


def kernel(
    owner, factors_hbm, stem_hbm, phase_hbm, out,
    factors, stem, phase, turned, recv, mixed, cosine, sine, own, raw0, raw1, slots, from_y, summed, from_z, full,
    high, low, send, land, a_send, a_land, b_send, b_land, x_land, c_land, local,
):
    row, col = lax.axis_index("row"), lax.axis_index("col")
    core, y, z_lo = row % 2, (row // 2) % 4, row // 8
    x, z_hi = col // 2, col % 2
    z = z_hi * 4 + z_lo

    def at_core(c):
        return (z_lo * 8 + y * 2 + c, col)

    def at_x(i):
        return (row, i * 2 + z_hi)

    def at_y(i):
        return (z_lo * 8 + i * 2 + core, col)

    def at_z(i):
        return ((i % 4) * 8 + y * 2 + core, x * 2 + i // 4)

    def row_peer(i):
        peer = ((z_lo + i % 4) % 4) * 8 + (row + i // 4) % 8
        return peer

    loads = [
        pltpu.make_async_copy(stem_hbm.at[0], stem.at[0], local.at[0]),
        pltpu.make_async_copy(stem_hbm.at[1], stem.at[1], local.at[1]),
        pltpu.make_async_copy(factors_hbm, factors, local.at[2]),
        pltpu.make_async_copy(phase_hbm, phase, local.at[3]),
    ]
    for load in loads:
        load.start()

    barrier = pltpu.get_barrier_semaphore()

    def greet(device):
        pl.semaphore_signal(barrier, inc=1, device_id=device, device_id_type=MESH)

    @pl.loop(1, N_ROW)
    def _(i):
        greet((row_peer(i), col))

    @pl.loop(1, NX)
    def _(i):
        greet(at_x((x + i) % NX))

    @pl.loop(0, NZ // 2)
    def _(i):
        greet(at_z((1 - z_hi) * 4 + i))

    for part in range(2):
        loads[part].wait()

        @pl.loop(0, 8)
        def _(a):
            for i in range(2):
                turned[part, i, pl.ds(a, 128, stride=8)] = stem[part, a, pl.ds(i * 128, 128)].T

    loads[2].wait()
    dot = functools.partial(jnp.dot, precision=lax.Precision.HIGHEST, preferred_element_type=F32)
    own[0] = dot(factors[0, 0], factors[1, 0]) - dot(factors[0, 1], factors[1, 1])
    own[1] = dot(factors[0, 0], factors[1, 1]) + dot(factors[0, 1], factors[1, 0])

    pl.semaphore_wait(barrier, N_ROW - 1 + NX - 1 + NZ // 2)

    def push(src, dst, stage, device):
        pltpu.make_async_remote_copy(
            src_ref=src, dst_ref=dst, send_sem=send.at[stage], recv_sem=land.at[stage],
            device_id=device, device_id_type=MESH,
        ).start()

    def stem_batch(index):
        @pl.loop(BATCHES[index], BATCHES[index + 1])
        def _(i):
            peer, b = row_peer(1 + i % PEERS), i // PEERS
            pltpu.make_async_remote_copy(
                src_ref=turned.at[:, :, pl.ds((peer * 4 + b) * 8, 8)],
                dst_ref=recv.at[:, b, :, pl.ds(row * 8, 8)],
                send_sem=a_send, recv_sem=a_land.at[b],
                device_id=(peer, col), device_id_type=MESH,
            ).start()

    push(own.at[1 - core], raw0.at[core], 0, at_core(1 - core))
    stem_batch(0)
    raw0[core] = own[core]
    for b in range(4):
        recv[:, b, :, pl.ds(row * 8, 8)] = turned[:, :, pl.ds((row * 4 + b) * 8, 8)]

    drained(raw0.at[0], land.at[0])

    @pl.loop(1, NX)
    def _(i):
        peer = (x + i) % NX
        push(raw0.at[:, pl.ds(peer * 64, 64)], raw1.at[x], 1, at_x(peer))

    stem_batch(1)
    raw1[x] = raw0[:, pl.ds(x * 64, 64)]
    loads[3].wait()

    @pl.loop(0, STEPS)
    def _(step):
        @pl.loop(0, 32)
        def _(i):
            angle = phase[step, pl.ds(i * 8, 8)]
            cosine[step, pl.ds(i * 8, 8)] = jnp.cos(angle)
            sine[step, pl.ds(i * 8, 8)] = jnp.sin(angle)

    drained(raw1.at[pl.ds(0, NX - 1)], land.at[1])
    for step in range(STEPS):
        at = owner[step]
        at_row, at_col = lax.shift_right_logical(at, 3), at & 7
        at_z_y = (at_col & 1) * 4 + lax.shift_right_logical(at_row, 3), lax.shift_right_logical(at_row, 1) & 3
        here = jnp.logical_and(at_z_y[0] == z, at_z_y[1] == y)
        value = raw1[lax.shift_right_logical(at_col, 1), at_row & 1]
        slots[step] = jnp.where(here, value, jnp.zeros_like(value))

    @pl.loop(1, NY)
    def _(i):
        peer = (y + i) % NY
        push(slots.at[:, pl.ds(peer * 16, 16)], from_y.at[y], 2, at_y(peer))

    stem_batch(2)
    from_y[y] = slots[:, pl.ds(y * 16, 16)]
    drained(from_y.at[pl.ds(0, NY - 1)], land.at[2])
    total = (from_y[0] + from_y[1]) + (from_y[2] + from_y[3])
    summed[...] = total.reshape(NZ, 8, 256)

    @pl.loop(1, NZ)
    def _(i):
        peer = (z + i) % NZ
        push(summed.at[peer], from_z.at[z], 3, at_z(peer))

    stem_batch(3)
    from_z[z] = summed[z]
    drained(from_z.at[pl.ds(0, NZ - 1)], land.at[3])
    total = from_z[0]
    for i in range(1, NZ):
        total = total + from_z[i]
    mine = full.at[:, core, x, y]
    eighth = full.at[z // 2, core, x, y, z % 2]
    eighth[...] = total

    @pl.loop(1, NZ)
    def _(i):
        push(eighth, eighth, 4, at_z((z + i) % NZ))

    stem_batch(4)
    drained(from_z.at[pl.ds(0, NZ - 1)], land.at[4])

    @pl.loop(1, NY)
    def _(i):
        push(mine, mine, 5, at_y((y + i) % NY))

    stem_batch(5)
    drained(from_y.at[pl.ds(0, NY - 1)], land.at[5])

    def pushed(part, sent, landed, device):
        pltpu.make_async_remote_copy(
            src_ref=part, dst_ref=part, send_sem=sent, recv_sem=landed,
            device_id=device, device_id_type=MESH,
        ).start()

    for step in range(STEPS):
        @pl.loop(1, NX)
        def _(i):
            pushed(full.at[step, core, x], send.at[6], x_land.at[step], at_x((x + i) % NX))

    stem_batch(6)

    def arrived(b):
        drained(turned.at[:, :, pl.ds(0, PEERS * 8)], a_land.at[b])
        return tuple(jnp.concatenate([recv[c, b, 0], recv[c, b, 1]], axis=1) for c in range(2))

    def prepare(step):
        drained(full.at[step, 1 - core], c_land.at[step])
        for part in range(2):
            branch = full[step, part].reshape(256, 256)
            if step % 2:
                branch = branch.T
            high[step, part], low[step, part] = split(branch)

    def advance(step, real, imag):
        xr, xi = split(real), split(imag)
        br = (high[step, 0], low[step, 0])
        bi = (high[step, 1], low[step, 1])
        if step % 2:
            yr = dot3(br, xr) - dot3(bi, xi)
            yi = dot3(bi, xr) + dot3(br, xi)
        else:
            yr = dot3(xr, br) - dot3(xi, bi)
            yi = dot3(xr, bi) + dot3(xi, br)
        return yr * cosine[step] - yi * sine[step], yr * sine[step] + yi * cosine[step]

    def send_off(b):
        pltpu.make_async_copy(
            mixed.at[b, :, pl.ds(row * 8, 8)], out.at[:, row * 4 + b], local.at[4]
        ).start()

        @pl.loop(1, N_ROW)
        def _(i):
            peer = row_peer(i)
            pltpu.make_async_remote_copy(
                src_ref=mixed.at[b, :, pl.ds(peer * 8, 8)],
                dst_ref=out.at[:, row * 4 + b],
                send_sem=b_send, recv_sem=b_land,
                device_id=(peer, col), device_id_type=MESH,
            ).start()

    def early(step):
        prepare(step)

        @pl.loop(0, EARLY)
        def _(b):
            if step == 0:
                real, imag = arrived(b)
            else:
                real, imag = mixed[b, 0], mixed[b, 1]
            mixed[b, 0], mixed[b, 1] = advance(step, real, imag)
            if step == STEPS - 1:
                send_off(b)

    for step in range(STEPS):
        drained(full.at[0, 0, pl.ds(0, NX - 1)], x_land.at[step])
        pushed(full.at[step, core], send.at[7], c_land.at[step], at_core(1 - core))
        if step:
            early(step - 1)
    early(STEPS - 1)

    @pl.loop(EARLY, 4)
    def _(b):
        real, imag = arrived(b)
        for step in range(STEPS):
            real, imag = advance(step, real, imag)
        mixed[b, 0], mixed[b, 1] = real, imag
        send_off(b)

    drained(out.at[:, pl.ds(0, 4)], local.at[4])
    drained(out.at[:, pl.ds(0, PEERS * 4)], b_land)
    drained(raw0.at[0], send.at[0])
    drained(raw1.at[pl.ds(0, NX - 1)], send.at[1])
    drained(from_y.at[pl.ds(0, NY - 1)], send.at[2])
    drained(from_z.at[pl.ds(0, NZ - 1)], send.at[3])
    drained(from_z.at[pl.ds(0, NZ - 1)], send.at[4])
    drained(from_y.at[pl.ds(0, NY - 1)], send.at[5])
    drained(full.at[pl.ds(0, NX - 1), 0], send.at[6])
    drained(full.at[:, 0], send.at[7])
    drained(turned.at[:, :, pl.ds(0, PEERS * 32)], a_send)
    drained(out.at[:, pl.ds(0, PEERS * 4)], b_send)


def on_device(stem_slab, factors, branch_owner, entangle_phase):
    vmem, dma = pltpu.VMEM, pltpu.SemaphoreType.DMA
    out = pl.pallas_call(
        kernel,
        out_shape=jax.ShapeDtypeStruct((2, 128, 8, 256), F32),
        in_specs=[
            pl.BlockSpec(memory_space=pltpu.SMEM),
            pl.BlockSpec(memory_space=pl.ANY),
            pl.BlockSpec(memory_space=pl.ANY),
            pl.BlockSpec(memory_space=pl.ANY),
        ],
        out_specs=pl.BlockSpec(memory_space=pl.ANY),
        scratch_shapes=[
            vmem((2, 2, 256, 256), F32),
            vmem((2, 8, 256, 128), F32),
            vmem((4, 256, 256), F32),
            vmem((2, 2, 1024, 128), F32),
            vmem((2, 4, 2, 256, 128), F32),
            vmem((4, 2, 256, 256), F32),
            vmem((4, 256, 256), F32),
            vmem((4, 256, 256), F32),
            vmem((2, 256, 256), F32),
            vmem((2, 256, 256), F32),
            vmem((4, 2, 64, 256), F32),
            vmem((4, 64, 256), F32),
            vmem((4, 4, 16, 256), F32),
            vmem((8, 8, 256), F32),
            vmem((8, 8, 256), F32),
            vmem((4, 2, 4, 4, 2, 8, 256), F32),
            vmem((4, 2, 256, 256), BF16),
            vmem((4, 2, 256, 256), BF16),
            dma((8,)), dma((8,)),
            dma(()), dma((4,)), dma(()), dma(()), dma((4,)), dma((4,)),
            dma((5,)),
        ],
        compiler_params=pltpu.CompilerParams(collective_id=0, has_side_effects=True),
    )(branch_owner, factors[0], stem_slab, entangle_phase)
    return out.transpose(0, 2, 3, 1)


def solution(mesh):
    return jax.shard_map(
        on_device,
        mesh=mesh,
        in_specs=(P(None, "row", None, "col"), P(("row", "col"), None, None, None, None), P(), P()),
        out_specs=P(None, "row", None, "col"),
        check_vma=False,
    )
```

```python
import functools

import jax
import jax.numpy as jnp
from jax import lax
from jax.experimental import pallas as pl
from jax.experimental.pallas import tpu as pltpu
from jax.sharding import PartitionSpec as P

MESH = pl.DeviceIdType.MESH
F32 = jnp.float32
BF16 = jnp.bfloat16
STEPS = 4

NX, NY, NZ, NC = 4, 4, 8, 2
N_ROW = 32
PEERS = N_ROW - 1
EARLY = 1
BATCHES = (0, 12, 36, 48, 60, 72, 90, 124)


def split(value):
    high = value.astype(BF16)
    return high, (value - high.astype(F32)).astype(BF16)


def dot3(left, right):
    (lh, ll), (rh, rl) = left, right
    dot = functools.partial(jnp.dot, preferred_element_type=F32)
    return dot(lh, rh) + (dot(lh, rl) + dot(ll, rh))


def drained(ref, sem):
    pltpu.make_async_copy(ref, ref, sem).wait()


def kernel(
    owner, factors_hbm, stem_hbm, phase_hbm, out,
    factors, stem, phase, turned, recv, mixed, cosine, sine, own, raw0, raw1, slots, from_y, summed, from_z, full,
    high, low, send, land, a_send, a_land, b_send, b_land, x_land, c_land, local, crossed, told,
):
    row, col = lax.axis_index("row"), lax.axis_index("col")
    core, y, z_lo = row % 2, (row // 2) % 4, row // 8
    x, z_hi = col // 2, col % 2
    z = z_hi * 4 + z_lo

    def at_core(c):
        return (z_lo * 8 + y * 2 + c, col)

    def at_x(i):
        return (row, i * 2 + z_hi)

    def at_y(i):
        return (z_lo * 8 + i * 2 + core, col)

    def at_z(i):
        return ((i % 4) * 8 + y * 2 + core, x * 2 + i // 4)

    def row_peer(i):
        peer = ((z_lo + i % 4) % 4) * 8 + (row + i // 4) % 8
        return peer

    loads = [
        pltpu.make_async_copy(stem_hbm.at[0], stem.at[0], local.at[0]),
        pltpu.make_async_copy(stem_hbm.at[1], stem.at[1], local.at[1]),
        pltpu.make_async_copy(factors_hbm, factors, local.at[2]),
        pltpu.make_async_copy(phase_hbm, phase, local.at[3]),
    ]
    for load in loads:
        load.start()

    barrier = pltpu.get_barrier_semaphore()

    def greet(device):
        pl.semaphore_signal(barrier, inc=1, device_id=device, device_id_type=MESH)

    @pl.loop(1, N_ROW)
    def _(i):
        greet((row_peer(i), col))

    @pl.loop(1, NX)
    def _(i):
        greet(at_x((x + i) % NX))

    middle = z_hi * 4 + z_lo == 3 + z_hi

    @pl.when(middle)
    def _():
        greet(at_z(4 - z_hi))

    for part in range(2):
        loads[part].wait()

        @pl.loop(0, 8)
        def _(a):
            for i in range(2):
                turned[part, i, pl.ds(a, 128, stride=8)] = stem[part, a, pl.ds(i * 128, 128)].T

    loads[2].wait()
    dot = functools.partial(jnp.dot, precision=lax.Precision.HIGHEST, preferred_element_type=F32)
    own[0] = dot(factors[0, 0], factors[1, 0]) - dot(factors[0, 1], factors[1, 1])
    own[1] = dot(factors[0, 0], factors[1, 1]) + dot(factors[0, 1], factors[1, 0])

    @pl.when(middle)
    def _():
        pl.semaphore_wait(barrier, N_ROW - 1 + NX - 1 + 1)
        pl.semaphore_signal(crossed, inc=1, device_id=at_z(4 - z_hi), device_id_type=MESH)

    @pl.when(jnp.logical_not(middle))
    def _():
        pl.semaphore_wait(barrier, N_ROW - 1 + NX - 1)

    def push(src, dst, stage, device):
        pltpu.make_async_remote_copy(
            src_ref=src, dst_ref=dst, send_sem=send.at[stage], recv_sem=land.at[stage],
            device_id=device, device_id_type=MESH,
        ).start()

    def pushed(part, sent, landed, device):
        pltpu.make_async_remote_copy(
            src_ref=part, dst_ref=part, send_sem=sent, recv_sem=landed,
            device_id=device, device_id_type=MESH,
        ).start()

    def stem_batch(index):
        @pl.loop(BATCHES[index], BATCHES[index + 1])
        def _(i):
            peer, b = row_peer(1 + i % PEERS), i // PEERS
            pltpu.make_async_remote_copy(
                src_ref=turned.at[:, :, pl.ds((peer * 4 + b) * 8, 8)],
                dst_ref=recv.at[:, b, :, pl.ds(row * 8, 8)],
                send_sem=a_send, recv_sem=a_land.at[b],
                device_id=(peer, col), device_id_type=MESH,
            ).start()

    push(own.at[1 - core], raw0.at[core], 0, at_core(1 - core))
    stem_batch(0)
    raw0[core] = own[core]
    for b in range(4):
        recv[:, b, :, pl.ds(row * 8, 8)] = turned[:, :, pl.ds((row * 4 + b) * 8, 8)]

    drained(raw0.at[0], land.at[0])

    @pl.loop(1, NX)
    def _(i):
        peer = (x + i) % NX
        push(raw0.at[:, pl.ds(peer * 64, 64)], raw1.at[x], 1, at_x(peer))

    stem_batch(1)
    raw1[x] = raw0[:, pl.ds(x * 64, 64)]
    loads[3].wait()

    @pl.loop(0, STEPS)
    def _(step):
        @pl.loop(0, 32)
        def _(i):
            angle = phase[step, pl.ds(i * 8, 8)]
            cosine[step, pl.ds(i * 8, 8)] = jnp.cos(angle)
            sine[step, pl.ds(i * 8, 8)] = jnp.sin(angle)

    drained(raw1.at[pl.ds(0, NX - 1)], land.at[1])

    @pl.when(middle)
    def _():
        pl.semaphore_wait(crossed, 1)

        @pl.loop(1, NZ // 2)
        def _(i):
            pl.semaphore_signal(told, inc=1, device_id=at_z(z_hi * 4 + (z_lo + i) % 4), device_id_type=MESH)

    for step in range(STEPS):
        at = owner[step]
        at_row, at_col = lax.shift_right_logical(at, 3), at & 7
        at_z_y = (at_col & 1) * 4 + lax.shift_right_logical(at_row, 3), lax.shift_right_logical(at_row, 1) & 3
        here = jnp.logical_and(at_z_y[0] == z, at_z_y[1] == y)
        value = raw1[lax.shift_right_logical(at_col, 1), at_row & 1]
        slots[step] = jnp.where(here, value, jnp.zeros_like(value))

    @pl.loop(1, NY)
    def _(i):
        peer = (y + i) % NY
        push(slots.at[:, pl.ds(peer * 16, 16)], from_y.at[y], 2, at_y(peer))

    stem_batch(2)
    from_y[y] = slots[:, pl.ds(y * 16, 16)]
    drained(from_y.at[pl.ds(0, NY - 1)], land.at[2])
    total = (from_y[0] + from_y[1]) + (from_y[2] + from_y[3])
    summed[...] = total.reshape(NZ, 8, 256)

    @pl.when(jnp.logical_not(middle))
    def _():
        pl.semaphore_wait(told, 1)

    @pl.loop(1, NZ)
    def _(i):
        peer = (z + i) % NZ
        push(summed.at[peer], from_z.at[z], 3, at_z(peer))

    stem_batch(3)
    from_z[z] = summed[z]
    drained(from_z.at[pl.ds(0, NZ - 1)], land.at[3])
    total = from_z[0]
    for i in range(1, NZ):
        total = total + from_z[i]
    mine = full.at[:, core, x, y]
    eighth = full.at[z // 2, core, x, y, z % 2]
    eighth[...] = total

    @pl.loop(1, NZ)
    def _(i):
        push(eighth, eighth, 4, at_z((z + i) % NZ))

    stem_batch(4)
    drained(from_z.at[pl.ds(0, NZ - 1)], land.at[4])

    @pl.loop(1, NY)
    def _(i):
        push(mine, mine, 5, at_y((y + i) % NY))

    for step in range(STEPS):
        @pl.loop(1, NX)
        def _(i):
            pushed(full.at[step, core, x, y], send.at[6], x_land.at[step], at_x((x + i) % NX))

    stem_batch(5)
    drained(from_y.at[pl.ds(0, NY - 1)], land.at[5])

    for step in range(STEPS):
        @pl.loop(1, NX)
        def _(i):
            for j in range(1, NY):
                pushed(full.at[step, core, x, (y + j) % NY], send.at[6], x_land.at[step], at_x((x + i) % NX))

    stem_batch(6)

    def arrived(b):
        drained(turned.at[:, :, pl.ds(0, PEERS * 8)], a_land.at[b])
        return tuple(jnp.concatenate([recv[c, b, 0], recv[c, b, 1]], axis=1) for c in range(2))

    def prepare(step):
        drained(full.at[step, 1 - core], c_land.at[step])
        for part in range(2):
            branch = full[step, part].reshape(256, 256)
            if step % 2:
                branch = branch.T
            high[step, part], low[step, part] = split(branch)

    def advance(step, real, imag):
        xr, xi = split(real), split(imag)
        br = (high[step, 0], low[step, 0])
        bi = (high[step, 1], low[step, 1])
        if step % 2:
            yr = dot3(br, xr) - dot3(bi, xi)
            yi = dot3(bi, xr) + dot3(br, xi)
        else:
            yr = dot3(xr, br) - dot3(xi, bi)
            yi = dot3(xr, bi) + dot3(xi, br)
        return yr * cosine[step] - yi * sine[step], yr * sine[step] + yi * cosine[step]

    def send_off(b):
        pltpu.make_async_copy(
            mixed.at[b, :, pl.ds(row * 8, 8)], out.at[:, row * 4 + b], local.at[4]
        ).start()

        @pl.loop(1, N_ROW)
        def _(i):
            peer = row_peer(i)
            pltpu.make_async_remote_copy(
                src_ref=mixed.at[b, :, pl.ds(peer * 8, 8)],
                dst_ref=out.at[:, row * 4 + b],
                send_sem=b_send, recv_sem=b_land,
                device_id=(peer, col), device_id_type=MESH,
            ).start()

    def early(step):
        prepare(step)

        @pl.loop(0, EARLY)
        def _(b):
            if step == 0:
                real, imag = arrived(b)
            else:
                real, imag = mixed[b, 0], mixed[b, 1]
            mixed[b, 0], mixed[b, 1] = advance(step, real, imag)
            if step == STEPS - 1:
                send_off(b)

    for step in range(STEPS):
        drained(full.at[0, 0, pl.ds(0, NX - 1)], x_land.at[step])
        pushed(full.at[step, core], send.at[7], c_land.at[step], at_core(1 - core))
        if step:
            early(step - 1)
    early(STEPS - 1)

    @pl.loop(EARLY, 4)
    def _(b):
        real, imag = arrived(b)
        for step in range(STEPS):
            real, imag = advance(step, real, imag)
        mixed[b, 0], mixed[b, 1] = real, imag
        send_off(b)

    drained(out.at[:, pl.ds(0, 4)], local.at[4])
    drained(out.at[:, pl.ds(0, PEERS * 4)], b_land)
    drained(raw0.at[0], send.at[0])
    drained(raw1.at[pl.ds(0, NX - 1)], send.at[1])
    drained(from_y.at[pl.ds(0, NY - 1)], send.at[2])
    drained(from_z.at[pl.ds(0, NZ - 1)], send.at[3])
    drained(from_z.at[pl.ds(0, NZ - 1)], send.at[4])
    drained(from_y.at[pl.ds(0, NY - 1)], send.at[5])
    drained(full.at[pl.ds(0, NX - 1), 0], send.at[6])
    drained(full.at[:, 0], send.at[7])
    drained(turned.at[:, :, pl.ds(0, PEERS * 32)], a_send)
    drained(out.at[:, pl.ds(0, PEERS * 4)], b_send)


def on_device(stem_slab, factors, branch_owner, entangle_phase):
    vmem, dma = pltpu.VMEM, pltpu.SemaphoreType.DMA
    out = pl.pallas_call(
        kernel,
        out_shape=jax.ShapeDtypeStruct((2, 128, 8, 256), F32),
        in_specs=[
            pl.BlockSpec(memory_space=pltpu.SMEM),
            pl.BlockSpec(memory_space=pl.ANY),
            pl.BlockSpec(memory_space=pl.ANY),
            pl.BlockSpec(memory_space=pl.ANY),
        ],
        out_specs=pl.BlockSpec(memory_space=pl.ANY),
        scratch_shapes=[
            vmem((2, 2, 256, 256), F32),
            vmem((2, 8, 256, 128), F32),
            vmem((4, 256, 256), F32),
            vmem((2, 2, 1024, 128), F32),
            vmem((2, 4, 2, 256, 128), F32),
            vmem((4, 2, 256, 256), F32),
            vmem((4, 256, 256), F32),
            vmem((4, 256, 256), F32),
            vmem((2, 256, 256), F32),
            vmem((2, 256, 256), F32),
            vmem((4, 2, 64, 256), F32),
            vmem((4, 64, 256), F32),
            vmem((4, 4, 16, 256), F32),
            vmem((8, 8, 256), F32),
            vmem((8, 8, 256), F32),
            vmem((4, 2, 4, 4, 2, 8, 256), F32),
            vmem((4, 2, 256, 256), BF16),
            vmem((4, 2, 256, 256), BF16),
            dma((8,)), dma((8,)),
            dma(()), dma((4,)), dma(()), dma(()), dma((4,)), dma((4,)),
            dma((5,)),
            pltpu.SemaphoreType.REGULAR, pltpu.SemaphoreType.REGULAR,
        ],
        compiler_params=pltpu.CompilerParams(collective_id=0, has_side_effects=True),
    )(branch_owner, factors[0], stem_slab, entangle_phase)
    return out.transpose(0, 2, 3, 1)


def solution(mesh):
    return jax.shard_map(
        on_device,
        mesh=mesh,
        in_specs=(P(None, "row", None, "col"), P(("row", "col"), None, None, None, None), P(), P()),
        out_specs=P(None, "row", None, "col"),
        check_vma=False,
    )
```
